32 devices in a mesh: dp: 32 (over z, y, x, core).
Axes of the slice: x: 2, y: 2, z: 4, core: 2. Of those that a mesh axis runs over, the one named last changes fastest.
Arguments:
- tokens: bfloat16 [4096, 2048], P('dp'), may hold values from -6 to 6
- cotangent: bfloat16 [4096, 2048], P('dp'), may hold values from -6 to 6
- seq_lengths: int32 [32, 4], P('dp'), may hold values from 1 to 125, as said below
- ln1_gain: bfloat16 [2048], P('dp'), may hold values from 0.25 to 1.75
- ln1_bias: bfloat16 [2048], P('dp'), may hold values from -1.5 to 1.5
- ln2_gain: bfloat16 [2048], P('dp'), may hold values from 0.25 to 1.75
- ln2_bias: bfloat16 [2048], P('dp'), may hold values from -1.5 to 1.5
- qkv_weight: bfloat16 [2048, 6144], P('dp'), may hold values from -0.125 to 0.125
- qkv_bias: bfloat16 [6144], P('dp'), may hold values from -3 to 9
- out_weight: bfloat16 [2048, 2048], P('dp'), may hold values from -0.5 to 0.5
- out_bias: bfloat16 [2048], P('dp'), may hold values from -1.5 to 1.5
- fc1_weight: bfloat16 [2048, 8192], P('dp'), may hold values from -0.125 to 0.125
- fc1_bias: bfloat16 [8192], P('dp'), may hold values from -2.5 to 2.5
- fc2_weight: bfloat16 [8192, 2048], P('dp'), may hold values from -0.0625 to 0.0625
- fc2_bias: bfloat16 [2048], P('dp'), may hold values from -1.5 to 1.5
Outputs:
- block_out: bfloat16 [4096, 2048], P('dp')
- input_grad: bfloat16 [4096, 2048], P('dp')
- ln1_gain_grad: float32 [2048], P('dp')
- ln1_bias_grad: float32 [2048], P('dp')
- ln2_gain_grad: float32 [2048], P('dp')
- ln2_bias_grad: float32 [2048], P('dp')
- qkv_weight_grad: float32 [2048, 6144], P('dp')
- qkv_bias_grad: float32 [6144], P('dp')
- out_weight_grad: float32 [2048, 2048], P('dp')
- out_bias_grad: float32 [2048], P('dp')
- fc1_weight_grad: float32 [2048, 8192], P('dp')
- fc1_bias_grad: float32 [8192], P('dp')
- fc2_weight_grad: float32 [8192, 2048], P('dp')
- fc2_bias_grad: float32 [2048], P('dp')
The draws below stay inside these ranges and needn't reach their ends.
Inputs may be any that keep to these rules, and one draw needn't show every extreme that they name: `seq_lengths`: row g holds the lengths of the 4 sequences of device g in order; their sum is 128 on every device, so no slot is padding.
All inputs are finite; a program needn't handle non-finite values.
Results may differ from the reference program's by a relative error of at most 0.015.
The reference program's roundings to bfloat16 on the way count: a program that leaves them out, or rounds other values in their place, can miss the bound.
Values may be sent and summed in bfloat16 or wider, within the bound.
No kernel may reach another device: no remote copies, remote signals or barrier semaphores. Data moves between devices by JAX's collectives and lax.ppermute only.
A program may use at most 384 MiB of HBM per device.

```python
import jax
import jax.numpy as jnp
from jax import lax

D = 2048
HEADS = 8
HEAD = 256
ROT = 64
FF = 8192
TOK_DEV = 128
BLOCK = 128
SLOTS = 4
GROUPS = 32
TOKENS = 4096


def draw_qkv_bias(key, part):
    values = jnp.clip(jax.random.normal(key, (3 * D,), jnp.float32) * 0.5, -3.0, 3.0)
    return values.astype(jnp.bfloat16)


def draw_seq_lengths(key, part):
    key_blocks = jax.random.fold_in(key, 11)
    key_full = jax.random.fold_in(key, 12)
    key_rest = jax.random.fold_in(key, 13)
    block_total = TOK_DEV // BLOCK
    blocks = jax.random.randint(key_blocks, (GROUPS,), 1, block_total + 1)
    full_index = jax.random.randint(key_full, (), 0, GROUPS)
    is_full = jnp.arange(GROUPS) == full_index
    blocks = jnp.where(is_full, block_total, blocks)
    live_count = blocks * BLOCK
    others = jax.random.randint(key_rest, (GROUPS, SLOTS - 1), 1, BLOCK // SLOTS + 1)
    others = jnp.where(is_full[:, None], 1, others)
    leading = live_count - jnp.sum(others, axis=1)
    return jnp.concatenate([leading[:, None], others], axis=1).astype(jnp.int32)


def levels(own_key, shape, split, smallest, high):
    gain = 1.0
    for dim, blocks in split:
        heights = jax.random.uniform(jax.random.fold_in(jax.random.fold_in(own_key, 6), dim), (blocks,), jnp.float32, smallest / len(split), high / len(split))
        gain = gain * jnp.repeat(jnp.exp(heights), shape[dim] // blocks).reshape((-1,) + (1,) * (len(shape) - 1 - dim))
    return gain


def centred(stream_key, shape, spread, reach, pieces=(), kind=jnp.bfloat16):
    entries = jax.random.normal(stream_key, shape, jnp.float32) * spread
    if len(pieces) > 0:
        entries = levels(stream_key, shape, pieces, -0.22, 0.18) * entries
    return jnp.clip(entries, min=-reach, max=reach).astype(kind)


def setup_inputs(seed: int = 0) -> dict:
    key_of = jax.random.split(jax.random.key(seed), 16)
    tokens = centred(key_of[0], (TOKENS, D), 1.0, 6.0, ((0, 32),))
    cotangent = centred(key_of[1], (TOKENS, D), 1.0, 6.0, ((0, 32),))
    seq_lengths = draw_seq_lengths(jax.random.fold_in(key_of[15], 71), 0)
    ln1_gain = jnp.clip(1.0 + 0.15 * jax.random.normal(key_of[3], (D,), jnp.float32), 0.25, 1.75).astype(jnp.bfloat16)
    ln1_bias = centred(key_of[4], (D,), 0.3, 1.5, ((0, 32),))
    ln2_gain = jnp.clip(1.0 + 0.15 * jax.random.normal(key_of[5], (D,), jnp.float32), 0.25, 1.75).astype(jnp.bfloat16)
    ln2_bias = centred(key_of[6], (D,), 0.3, 1.5, ((0, 32),))
    qkv_weight = centred(key_of[7], (D, 3 * D), D ** -0.5, 0.125, ((0, 32),))
    qkv_bias = draw_qkv_bias(jax.random.fold_in(key_of[15], 71), 0)
    out_weight = centred(key_of[9], (D, D), (D // 16) ** -0.5, 0.5, ((0, 32),))
    out_bias = centred(key_of[10], (D,), 0.3, 1.5, ((0, 32),))
    fc1_weight = centred(key_of[11], (D, FF), D ** -0.5, 0.125, ((0, 32),))
    fc1_bias = centred(key_of[12], (FF,), 0.5, 2.5, ((0, 32),))
    fc2_weight = centred(key_of[13], (FF, D), FF ** -0.5, 0.0625, ((0, 32),))
    fc2_bias = centred(key_of[14], (D,), 0.3, 1.5, ((0, 32),))
    return dict(tokens=tokens, cotangent=cotangent, seq_lengths=seq_lengths, ln1_gain=ln1_gain, ln1_bias=ln1_bias, ln2_gain=ln2_gain, ln2_bias=ln2_bias, qkv_weight=qkv_weight, qkv_bias=qkv_bias, out_weight=out_weight, out_bias=out_bias, fc1_weight=fc1_weight, fc1_bias=fc1_bias, fc2_weight=fc2_weight, fc2_bias=fc2_bias)


@jax.custom_vjp
def low(v):
    return lax.optimization_barrier(v.astype(jnp.bfloat16)).astype(jnp.float32)

@jax.custom_vjp
def low_back(v):
    return v

def low_keep(v):
    return (low(v), None)

def low_pass(kept, grad):
    return (grad,)

def back_keep(v):
    return (v, None)

def back_low(kept, grad):
    return (low(grad),)
low.defvjp(low_keep, low_pass)
low_back.defvjp(back_keep, back_low)

def norm_rows(values):
    row_mean = lax.optimization_barrier(jnp.mean(values, axis=-1, keepdims=True))
    centered = values - row_mean
    row_var = lax.optimization_barrier(jnp.mean(centered * centered, axis=-1, keepdims=True))
    return centered * lax.rsqrt(row_var + 1e-05)

def seq_layout(lengths_row, row_count):
    ends_at = jnp.cumsum(lengths_row).astype(jnp.int32)
    starts = (ends_at - lengths_row).astype(jnp.int32)
    indices = jnp.arange(row_count, dtype=jnp.int32)
    segment = lax.optimization_barrier(jnp.sum((indices[:, None] >= ends_at[None, :]).astype(jnp.int32), axis=1)).astype(jnp.int32)
    onehot = segment[:, None] == jnp.arange(lengths_row.shape[0], dtype=jnp.int32)[None, :]
    position = indices - lax.optimization_barrier(jnp.sum(jnp.where(onehot, starts[None, :], 0), axis=1)).astype(jnp.int32)
    return (segment, position, indices)

def rotate(vector_in, position):
    half_rot = ROT // 2
    frequency = 10000.0 ** (-(jnp.arange(half_rot, dtype=jnp.float32) * 2.0) / ROT)
    angle_row = position.astype(jnp.float32)[:, None] * frequency[None, :]
    cosine = jnp.concatenate([jnp.cos(angle_row), jnp.cos(angle_row)], axis=1)[:, None, :]
    sine_row = jnp.concatenate([jnp.sin(angle_row), jnp.sin(angle_row)], axis=1)[:, None, :]
    turned = vector_in[..., :ROT]
    turned_half = jnp.concatenate([-turned[..., half_rot:], turned[..., :half_rot]], axis=-1)
    return jnp.concatenate([turned * cosine + turned_half * sine_row, vector_in[..., ROT:]], axis=-1)

def attend_group(query, key_part, value_part, lengths_row):
    segment, position, indices = seq_layout(lengths_row, TOK_DEV)
    q_low = low(rotate(query, position))
    k_low = low(rotate(key_part, position))
    v_low = low(value_part)
    scores = jnp.einsum('ihd,jhd->hij', q_low, k_low, precision=lax.Precision.HIGHEST) * HEAD ** (-0.5)
    scores = low_back(scores)
    allowed = (segment[:, None] == segment[None, :]) & (indices[None, :] <= indices[:, None])
    scores = jnp.where(allowed[None], scores, -1e+30)
    probs_low = low(jax.nn.softmax(scores, axis=-1))
    return jnp.einsum('hij,jhd->ihd', probs_low, v_low, precision=lax.Precision.HIGHEST)

def forward(tokens_f, gain_one, bias_one, gain_two, bias_two, w_qkv, bias_qkv, w_out, bias_out, w_fc1, bias_fc1, w_fc2, bias_fc2, seq_lengths):
    precise = lax.Precision.HIGHEST
    live_rows = jnp.arange(TOK_DEV, dtype=jnp.int32)[None, :] < lax.optimization_barrier(jnp.sum(seq_lengths, axis=1)).astype(jnp.int32)[:, None]
    live_f = live_rows.reshape(TOKENS, 1).astype(jnp.float32)
    normed = norm_rows(tokens_f)
    first_low = low(normed * gain_one + bias_one)
    second_low = low(normed * gain_two + bias_two)
    qkv_full = low_back(jnp.dot(first_low, w_qkv, precision=precise) + bias_qkv)
    grouped = qkv_full.reshape(GROUPS, TOK_DEV, HEADS, 3, HEAD)
    checked = jax.checkpoint(attend_group)

    def group_step(group_data):
        return checked(group_data[0], group_data[1], group_data[2], group_data[3])
    context = lax.map(group_step, (grouped[:, :, :, 0], grouped[:, :, :, 1], grouped[:, :, :, 2], seq_lengths))
    context = low_back(low(context.reshape(TOKENS, D)))
    attn_out = jnp.dot(context, w_out, precision=precise) + bias_out
    gelu_in = low_back(jnp.dot(second_low, w_fc1, precision=precise) + bias_fc1)
    act_low = low(jax.nn.gelu(gelu_in, approximate=False))
    mlp_out = jnp.dot(act_low, w_fc2, precision=precise) + bias_fc2
    return (tokens_f + attn_out + mlp_out) * live_f

def reference(tokens, cotangent, seq_lengths, ln1_gain, ln1_bias, ln2_gain, ln2_bias, qkv_weight, qkv_bias, out_weight, out_bias, fc1_weight, fc1_bias, fc2_weight, fc2_bias):
    values = [tokens, ln1_gain, ln1_bias, ln2_gain, ln2_bias, qkv_weight, qkv_bias, out_weight, out_bias, fc1_weight, fc1_bias, fc2_weight, fc2_bias]
    values = [item.astype(jnp.float32) for item in values]

    def forward_all(*inputs):
        return forward(*inputs, seq_lengths)
    block_value, pullback = jax.vjp(forward_all, *values)
    gradients = pullback(cotangent.astype(jnp.float32))
    return (block_value.astype(jnp.bfloat16), gradients[0].astype(jnp.bfloat16), gradients[1], gradients[2], gradients[3], gradients[4], gradients[5], gradients[6], gradients[7], gradients[8], gradients[9], gradients[10], gradients[11], gradients[12])
```

```python
import jax
import jax.numpy as jnp
from jax import lax
from jax.sharding import PartitionSpec as P

HEADS = 8
ROT = 64
GROUP = 32
BF = jnp.bfloat16
F32 = jnp.float32


def dot(left, right):
    return jnp.dot(left, right, preferred_element_type=F32)


def dot_rows(left, right):
    return lax.dot_general(left, right, (((0,), (0,)), ((), ())), preferred_element_type=F32)


def dot_cols(left, right):
    return lax.dot_general(left, right, (((1,), (1,)), ((), ())), preferred_element_type=F32)


def row_stats(values):
    row_mean = jnp.mean(values, axis=-1, keepdims=True)
    centered = values - row_mean
    row_var = jnp.mean(centered * centered, axis=-1, keepdims=True)
    rstd = lax.rsqrt(row_var + 1e-05)
    return centered * rstd, rstd


def seq_layout(lengths, rows):
    ends = jnp.cumsum(lengths, axis=1)
    starts = ends - lengths
    indices = jnp.arange(rows, dtype=jnp.int32)
    past = (indices[None, :, None] >= ends[:, None, :]).astype(jnp.int32)
    segment = jnp.sum(past, axis=2)
    slot = jnp.arange(lengths.shape[1], dtype=jnp.int32)
    onehot = segment[:, :, None] == slot[None, None, :]
    position = indices[None, :] - jnp.sum(jnp.where(onehot, starts[:, None, :], 0), axis=2)
    return segment, position, indices


def rotary_tables(position):
    half = ROT // 2
    frequency = 10000.0 ** (-(jnp.arange(half, dtype=F32) * 2.0) / ROT)
    angle = position.astype(F32)[..., None] * frequency
    return jnp.cos(angle), jnp.sin(angle)


def rotate(values, cosine, sine):
    half = ROT // 2
    lo = values[..., :half]
    hi = values[..., half:ROT]
    return jnp.concatenate(
        [lo * cosine - hi * sine, hi * cosine + lo * sine, values[..., ROT:]], axis=-1
    )


def gelu_parts(values):
    cdf = 0.5 * (1.0 + lax.erf(values * 0.7071067811865476))
    pdf = jnp.exp(-0.5 * values * values) * 0.3989422804014327
    return values * cdf, cdf + values * pdf


def solution(mesh):
    count = mesh.shape["dp"]
    outer = count // GROUP

    def flat(pair_of):
        return [(i, (i // GROUP) * GROUP + pair_of(i % GROUP)) for i in range(count)]

    swap_core = flat(lambda b: b ^ 1)
    swap_x = flat(lambda b: b ^ 2)
    swap_two = flat(lambda b: b ^ (4 if b % 2 == 0 else 2))
    swap_three = flat(lambda b: b ^ (2 if b % 2 == 0 else 4))
    swap_z1 = flat(lambda b: b ^ 8)
    swap_z2 = flat(lambda b: b ^ 16)
    inner_groups = [[a * GROUP + b for b in range(GROUP)] for a in range(outer)]
    outer_groups = [[a * GROUP + b for a in range(outer)] for b in range(GROUP)]

    def send(values, pairs):
        return lax.ppermute(values, "dp", pairs)

    def gather_outer(values):
        if outer == 1:
            return values[None]
        return lax.all_gather(values, "dp", axis=0, axis_index_groups=outer_groups)

    def scatter_outer(values):
        if outer == 1:
            return values[0]
        return lax.psum_scatter(
            values, "dp", scatter_dimension=0, axis_index_groups=outer_groups, tiled=False
        )

    def exchange(values):
        return lax.all_to_all(
            values, "dp", 0, 0, axis_index_groups=inner_groups if outer > 1 else None, tiled=True
        )

    def on_device(
        tokens, cotangent, seq_lengths, ln1_gain, ln1_bias, ln2_gain, ln2_bias,
        qkv_weight, qkv_bias, out_weight, out_bias, fc1_weight, fc1_bias, fc2_weight, fc2_bias,
    ):
        rows, width = tokens.shape
        slots = seq_lengths.shape[1]
        own = width // count
        hidden = fc1_weight.shape[1]
        per = hidden // count
        head = width // HEADS
        quad = GROUP // HEADS
        member = lax.axis_index("dp") % GROUP
        core = member % 2
        bit = [(member // (1 << k)) % 2 for k in range(5)]
        scale = head ** (-0.5)

        both = jnp.concatenate([tokens, cotangent], axis=0)
        plane = [both]
        plane.append(send(both, swap_z1))
        plane.append(send(both, swap_z2))
        plane.append(send(plane[2], swap_z1))

        small = jnp.concatenate(
            [ln1_gain, ln1_bias, ln2_gain, ln2_bias, out_bias, fc2_bias,
             qkv_bias, fc1_bias, seq_lengths[0].astype(BF)]
        )
        pad = (-small.shape[0]) % 128
        small = jnp.pad(small, (0, pad))[None]
        for k in range(5):
            other = send(small, flat(lambda b, k=k: b ^ (1 << k)))
            low = jnp.where(bit[k] == 0, small, other)
            high = jnp.where(bit[k] == 0, other, small)
            small = jnp.concatenate([low, high], axis=0)
        group_small = small
        every = gather_outer(small)

        def whole(start, size):
            return every[:, :, start : start + size].reshape(-1)

        gain_one = whole(0, own).astype(F32)
        bias_one = whole(own, own).astype(F32)
        gain_two = whole(2 * own, own).astype(F32)
        bias_two = whole(3 * own, own).astype(F32)
        end_bias = whole(4 * own, own).astype(F32) + whole(5 * own, own).astype(F32)
        at = 6 * own
        wide = qkv_bias.shape[0]
        bias_qkv_all = whole(at, wide).reshape(HEADS, 3 * head)
        at += wide
        bias_fc1_all = every[:, :, at : at + per]
        at += per
        lengths = group_small[:, at : at + slots].astype(jnp.int32)

        my_head = member // quad
        bias_qkv = lax.dynamic_index_in_dim(bias_qkv_all, my_head, 0, keepdims=False).astype(F32)
        mine_bias = lax.dynamic_index_in_dim(bias_fc1_all, member, 1, keepdims=False).reshape(-1)
        other_bias = lax.dynamic_index_in_dim(
            bias_fc1_all, member + 1 - 2 * core, 1, keepdims=False
        ).reshape(-1)
        bias_fc1 = jnp.concatenate([mine_bias, other_bias]).astype(F32)

        part = 3 * head // 2
        fpart = outer * per
        fc1_blocks = fc1_weight.reshape(own, outer, GROUP, per)
        fc1_blocks = jnp.transpose(fc1_blocks, (2, 0, 1, 3)).reshape(GROUP, own, fpart)
        qkv_blocks = qkv_weight.reshape(own, HEADS, 1, 2, part)
        qkv_blocks = jnp.broadcast_to(qkv_blocks, (own, HEADS, quad // 2, 2, part))
        qkv_blocks = jnp.transpose(qkv_blocks, (1, 2, 3, 0, 4)).reshape(GROUP, own, part)
        moved = exchange(jnp.concatenate([fc1_blocks, qkv_blocks], axis=2))
        moved = gather_outer(moved.reshape(GROUP * own, -1)).reshape(width, -1)
        moved_other = send(moved, swap_core)
        w_fc1 = jnp.concatenate([moved[:, :fpart], moved_other[:, :fpart]], axis=1)
        halves = [moved[:, fpart:], moved_other[:, fpart:]]
        w_qkv = jnp.concatenate(
            [jnp.where(core == 0, halves[0], halves[1]), jnp.where(core == 0, halves[1], halves[0])],
            axis=1,
        )
        fc2_mine = gather_outer(fc2_weight).reshape(fpart, width)
        w_fc2 = jnp.concatenate([fc2_mine, send(fc2_mine, swap_core)], axis=0)
        if outer == 1:
            other = send(out_weight, swap_core)
            pair = jnp.concatenate(
                [jnp.where(core == 0, out_weight, other), jnp.where(core == 0, other, out_weight)]
            )
            other = send(pair, swap_x)
            w_out = jnp.concatenate(
                [jnp.where(bit[1] == 0, pair, other), jnp.where(bit[1] == 0, other, pair)]
            )
        else:
            w_out = lax.all_gather(out_weight, "dp", axis=0, tiled=True)
            w_out = lax.dynamic_slice_in_dim(w_out, my_head * head, head, 0)

        chunks = []
        for piece in plane:
            two = send(piece, swap_two)
            three = send(piece, swap_three)
            four = send(two, swap_three)
            chunks.append((piece, two, three, four))

        def mlp(values, grad):
            normed, _ = row_stats(values.astype(F32))
            second = (normed * gain_two + bias_two).astype(BF)
            gelu_in = dot(second, w_fc1) + bias_fc1
            act, slope = gelu_parts(gelu_in)
            act_low = act.astype(BF)
            out = dot(act_low, w_fc2)
            d_gelu = (dot_cols(grad, w_fc2) * slope).astype(BF)
            d_second = dot_cols(d_gelu, w_fc1)
            sums = (
                dot_rows(second, d_gelu),
                dot_rows(act_low, grad),
                jnp.sum(d_gelu.astype(F32), axis=0),
                jnp.sum(d_second * normed, axis=0),
                jnp.sum(d_second, axis=0),
                jnp.sum(grad.astype(F32), axis=0),
            )
            return out, d_second * gain_two, sums

        def attend(values, grad, lens):
            total = values.shape[0]
            groups = total // rows
            normed, _ = row_stats(values.astype(F32))
            first = (normed * gain_one + bias_one).astype(BF)
            qkv = (dot(first, w_qkv) + bias_qkv).reshape(groups, rows, 3, head)
            segment, position, indices = seq_layout(lens, rows)
            cosine, sine = rotary_tables(position)
            q_low = rotate(qkv[:, :, 0], cosine, sine).astype(BF)
            k_low = rotate(qkv[:, :, 1], cosine, sine).astype(BF)
            v_low = qkv[:, :, 2].astype(BF)
            allowed = (segment[:, :, None] == segment[:, None, :]) & (
                indices[None, None, :] <= indices[None, :, None]
            )

            def prod(spec, left, right):
                return jnp.einsum(spec, left, right, preferred_element_type=F32)

            scores = jnp.where(allowed, prod("gid,gjd->gij", q_low, k_low) * scale, -1e30)
            exps = jnp.exp(scores - jnp.max(scores, axis=-1, keepdims=True))
            probs = exps / jnp.sum(exps, axis=-1, keepdims=True)
            probs_low = probs.astype(BF)
            context = prod("gij,gjd->gid", probs_low, v_low).astype(BF).reshape(total, head)
            out = dot(context, w_out)
            d_context = dot_cols(grad, w_out).astype(BF)
            d_ctx = d_context.reshape(groups, rows, head)
            d_probs = prod("gid,gjd->gij", d_ctx, v_low)
            inner = jnp.sum(probs * d_probs, axis=-1, keepdims=True)
            d_scores = (probs * (d_probs - inner)).astype(BF)
            d_query = prod("gij,gjd->gid", d_scores, k_low) * scale
            d_key = prod("gij,gid->gjd", d_scores, q_low) * scale
            d_value = prod("gij,gid->gjd", probs_low, d_ctx)
            d_qkv = jnp.concatenate(
                [rotate(d_query, cosine, -sine), rotate(d_key, cosine, -sine), d_value], axis=-1
            )
            d_qkv = d_qkv.astype(BF).reshape(total, 3 * head)
            d_first = dot_cols(d_qkv, w_qkv)
            sums = (
                dot_rows(first, d_qkv),
                dot_rows(context, grad),
                jnp.sum(d_qkv.astype(F32), axis=0),
                jnp.sum(d_first * normed, axis=0),
                jnp.sum(d_first, axis=0),
            )
            return out, d_first * gain_one, sums

        mlp_sums = None
        att_sums = None
        reduced = [None] * 4
        for k in (1, 2, 3, 0):
            shards = chunks[k]
            values = jnp.concatenate([s[:rows] for s in shards])
            grad = jnp.concatenate([s[rows:] for s in shards])
            side = jnp.where(core == 0, shards[1], shards[2])
            base = member ^ (8 * k)
            lens = jnp.stack(
                [
                    lax.dynamic_index_in_dim(lengths, base, 0, keepdims=False),
                    lax.dynamic_index_in_dim(lengths, base ^ 4, 0, keepdims=False),
                ]
            )
            a_out, a_dn, sums = attend(
                jnp.concatenate([shards[0][:rows], side[:rows]]),
                jnp.concatenate([shards[0][rows:], side[rows:]]),
                lens,
            )
            att_sums = sums if att_sums is None else tuple(p + q for p, q in zip(att_sums, sums))
            m_out, m_dn, sums = mlp(values, grad)
            mlp_sums = sums if mlp_sums is None else tuple(p + q for p, q in zip(mlp_sums, sums))

            def merged(m, a):
                m = m.reshape(4, rows, width)
                a = a.reshape(2, rows, width)
                return (
                    m[0] + a[0],
                    m[1] + jnp.where(core == 0, a[1], 0.0),
                    m[2] + jnp.where(core == 0, 0.0, a[1]),
                    m[3],
                )

            out = merged(m_out, a_out)
            dn = merged(m_dn, a_dn)
            got = send(jnp.concatenate([out[2], dn[2], out[3], dn[3]]).astype(BF), swap_three)
            got = got.astype(F32)
            keep = jnp.concatenate([out[0], dn[0]]) + got[: 2 * rows]
            give = jnp.concatenate([out[1], dn[1]]) + got[2 * rows :]
            reduced[k] = keep + send(give.astype(BF), swap_two).astype(F32)

        far = reduced[2] + send(reduced[3].astype(BF), swap_z1).astype(F32)
        near = reduced[0] + send(reduced[1].astype(BF), swap_z1).astype(F32)
        done = near + send(far.astype(BF), swap_z2).astype(F32)

        tok = tokens.astype(F32)
        block_out = (tok + done[:rows] + end_bias).astype(BF)
        d_normed = done[rows:]
        normed, rstd = row_stats(tok)
        inner = jnp.mean(d_normed * normed, axis=-1, keepdims=True)
        mean = jnp.mean(d_normed, axis=-1, keepdims=True)
        input_grad = (
            cotangent.astype(F32) + (d_normed - mean - normed * inner) * rstd
        ).astype(BF)

        g_fc1, g_fc2, g_bfc1, g_gain2, g_bias2, col_sum = mlp_sums
        g_qkv, g_out, g_bqkv, g_gain1, g_bias1 = att_sums
        g_fc1 = g_fc1[:, :fpart] + send(g_fc1[:, fpart:], swap_core)
        g_fc2 = g_fc2[:fpart] + send(g_fc2[fpart:], swap_core)
        d_fc2 = scatter_outer(g_fc2.reshape(outer, per, width))

        def halve(values, which, pairs, axis):
            low, high = jnp.split(values, 2, axis=axis)
            keep = jnp.where(which == 0, low, high)
            give = jnp.where(which == 0, high, low)
            return keep + send(give, pairs)

        g_qkv = halve(g_qkv, core, swap_core, 1)
        g_qkv = halve(g_qkv, bit[1], swap_x, 1)
        if outer == 1:
            rows_out = jnp.swapaxes(g_out.reshape(2, 2, own, width), 0, 1)
            rows_out = halve(rows_out, core, swap_core, 0)[0]
            d_out = halve(rows_out, bit[1], swap_x, 0)[0]
        else:
            full = jnp.zeros((width, width), F32)
            full = lax.dynamic_update_slice_in_dim(full, g_out, my_head * head, 0)
            d_out = lax.psum_scatter(full, "dp", scatter_dimension=0, tiled=True)

        part = part // 2
        blocks = jnp.concatenate([g_fc1, g_qkv], axis=1)
        blocks = scatter_outer(blocks.reshape(outer, GROUP * own, fpart + part))

        v_qkv = lax.dynamic_update_slice(jnp.zeros((HEADS, 3 * head), F32), g_bqkv[None], (my_head, 0))
        v_fc1 = g_bfc1.reshape(2, outer, 1, per)
        v_fc1 = jnp.where(core == 0, v_fc1, v_fc1[::-1])
        v_fc1 = jnp.concatenate([v_fc1[0], v_fc1[1]], axis=1)
        v_fc1 = lax.dynamic_update_slice(
            jnp.zeros((outer, GROUP, per), F32), v_fc1, (0, member - core, 0)
        )
        v_out = jnp.zeros((outer, GROUP, own), F32)
        col_part = lax.dynamic_slice_in_dim(col_sum.reshape(outer, GROUP, own), member - core, 2, 1)
        v_out = lax.dynamic_update_slice(v_out, col_part, (0, member - core, 0))
        vectors = jnp.concatenate(
            [v.reshape(outer, GROUP, -1) for v in (g_gain1, g_bias1, g_gain2, g_bias2, v_out, v_qkv, v_fc1)],
            axis=2,
        )
        vectors = scatter_outer(vectors)
        size = vectors.shape[1]
        lanes = fpart + part
        extra = -(-size // lanes)
        vectors = jnp.pad(vectors, ((0, 0), (0, extra * lanes - size)))
        packed = jnp.concatenate(
            [blocks.reshape(GROUP, own, lanes), vectors.reshape(GROUP, extra, lanes)], axis=1
        )
        packed = exchange(packed)
        vec = jnp.sum(packed[:, own:], axis=0).reshape(-1)
        packed = packed[:, :own]
        d_fc1 = packed[:, :, :fpart].reshape(GROUP, own, outer, per)
        d_fc1 = jnp.transpose(d_fc1, (1, 2, 0, 3)).reshape(own, hidden)
        d_qkv = packed[:, :, fpart:].reshape(HEADS, quad // 2, 2, own, part)
        d_qkv = jnp.transpose(d_qkv, (3, 0, 2, 1, 4)).reshape(own, 3 * width)
        d_g1, d_b1, d_g2, d_b2, d_bout = (vec[i * own : (i + 1) * own] for i in range(5))
        at = 5 * own
        d_bqkv = vec[at : at + wide]
        d_bfc1 = vec[at + wide : at + wide + per]
        return (
            block_out, input_grad, d_g1, d_b1, d_g2, d_b2, d_qkv, d_bqkv,
            d_out, d_bout, d_fc1, d_bfc1, d_fc2, d_bout,
        )

    split = P("dp", None)
    line = P("dp")
    in_specs = (
        split, split, split, line, line, line, line, split, line, split, line, split, line, split, line,
    )
    out_specs = (
        split, split, line, line, line, line, split, line, split, line, split, line, split, line,
    )
    return jax.shard_map(
        on_device, mesh=mesh, in_specs=in_specs, out_specs=out_specs, check_vma=False
    )
```
